32 devices in a mesh: groups: 2 (over y), space: 4 (over z), phase: 4 (over x, core).
Axes of the slice: x: 2, y: 2, z: 4, core: 2. Of those that a mesh axis runs over, the one named last changes fastest.
Arguments:
- intensity: float32 [16, 131072], P('phase', ('groups', 'space')), parts along dimension 1, may hold values from -6 to 6
- image_grad: bfloat16 [3, 16, 131072], P(None, 'phase', ('groups', 'space')), parts along dimension 2, may hold values from -6 to 6
- owner: int32 [131072, 1], P(('groups', 'space')), parts along dimension 0, may hold values from 0 to 3; in each aligned block of 16384 rows (0 to 16383, 16384 to 32767, ...) at most 8192 rows name the same one
- coord_xy: int32 [2, 131072], P(None, ('groups', 'space')), parts along dimension 1, may hold values from 0 to 463
- coord_z: int32 [131072], P(('groups', 'space')), parts along dimension 0, may hold values from 0 to 127
Outputs:
- control_grad: float32 [6, 16, 32, 1024], P('groups', 'phase', 'space'), parts along dimension 0
The draws below stay inside these ranges and needn't reach their ends.
There are 2 independent parts, one for each index of `groups`. The reference program is written for one: setup_inputs(seed, part) draws one part's arguments, and reference() takes and returns one part's arrays. A program takes and returns all parts, laid end to end along the dimension named above; each array names one. Nothing has to cross between parts.
Inputs may be any that keep to these rules, and one draw needn't show every extreme that they name: Of the samples of one device, at most 8192 name the same owner, and some device has exactly 8192 samples for some owner.
All inputs are finite; a program needn't handle non-finite values.
Results may differ from the reference program's by a relative error of at most 0.0041.
Values sent between devices are 32-bit elements; how exact they have to be, the bound alone decides.
No kernel may reach another device: no remote copies, remote signals or barrier semaphores. Data moves between devices by JAX's collectives and lax.ppermute only.
A program may use at most 64 MiB of HBM per device.

```python
import math
import jax
import jax.numpy as jnp
import numpy as np
from jax import lax

P_SIZE = 16
GX = 32
SPC = 16
GZ_DEV = 8
S_DEV = 16384
CAP = 8192
NSAMP = 65536
NZC = 32
N_SPACE = 4


def set_ends(result, stream_key, low, high):
    longest = result.shape.index(max(result.shape))
    spots = []
    for shift in (0, 1):
        where = [jax.random.randint(jax.random.fold_in(stream_key, axis), (), 0, length) for axis, length in enumerate(result.shape)]
        where[longest] = (where[longest] + shift) % result.shape[longest]
        spots.append(tuple(where))
    return result.at[spots[0]].set(low).at[spots[1]].set(high)


def levels(rng, dims, split, smallest, high):
    level, own = 1.0, jax.random.fold_in(rng, 6)
    for dim, shards_of in split:
        steps = jnp.exp(jax.random.uniform(jax.random.fold_in(own, dim), (shards_of,), jnp.float32, smallest / len(split), high / len(split)))
        level = level * jnp.repeat(steps, dims[dim] // shards_of).reshape([-1 if axis == dim else 1 for axis in range(len(dims))])
    return level


def routed_block(rng, own, number, rows, amount, top, bound, skew):
    sequence = jax.random.permutation(rng, amount)
    crowded, usual = portions_of(amount, rows * top, bound, skew, True), portions_of(amount, rows * top, bound, skew, False)
    places = jnp.arange(amount)

    def named(sizes, rotation):
        used = int((sizes > 0).sum())
        fixed = max(1, used // 4)
        moved = fixed + (places - fixed + rotation * (used - fixed)) % max(1, amount - fixed)
        return jnp.zeros((amount,), jnp.int32).at[sequence[jnp.where(places < fixed, places, moved)]].set(jnp.asarray(sizes, jnp.int32))

    sizes = jnp.where(number % 4 == 0, named(crowded, number // 4), named(usual, number - number // 4 - 1))
    mixed = jax.random.permutation(jax.random.fold_in(own, 3), amount)
    giver, taker = mixed[0:amount // 2 * 2:2], mixed[1:amount // 2 * 2:2]
    margin = jnp.minimum(sizes[giver] - 1, bound - sizes[taker]) // 2
    margin = jnp.where((giver == sequence[0]) | (taker == sequence[0]) | (sizes[taker] == 0), 0, jnp.maximum(margin, 0))
    moved = jax.random.randint(jax.random.fold_in(own, 4), (amount // 2,), 0, 1 << 20) % (margin + 1)
    sizes = sizes.at[giver].add(-moved).at[taker].add(moved)
    labels = jnp.searchsorted(jnp.cumsum(sizes), jnp.arange(rows * top), side="right").astype(jnp.int32)
    listing = labels.reshape(top, rows).T
    listing = listing[jax.random.permutation(jax.random.fold_in(own, 1), rows)]
    rotation = jax.random.randint(jax.random.fold_in(own, 2), (rows, 1), 0, top)
    return jnp.take_along_axis(listing, (jnp.arange(top)[None, :] + rotation) % top, axis=1)


def portions_of(number_of, total, reach, skew, full):
    weights = [(1 << 20) // math.isqrt(rank ** skew) + 1 for rank in range(1, number_of + 1)]
    largest = reach if full else min(reach, max(-(-total // number_of), total * weights[0] // sum(weights)))
    least = 1 if total - largest >= number_of - 1 else 0
    holding, surplus = [largest] + [least] * (number_of - 1), total - largest - least * (number_of - 1)
    while surplus > 0:
        free = [i for i in range(1, number_of) if holding[i] < largest] or [i for i in range(1, number_of) if holding[i] < reach]
        pool, left = sum([weights[i] for i in free]), surplus
        for i in free:
            more = min(reach - holding[i], max(1, left * weights[i] // pool), surplus)
            holding[i] = holding[i] + more
            surplus = surplus - more
    return np.array(holding)


def gaussian(rng, shape, scale, bound, shards=(), kind=jnp.bfloat16):
    level = levels(rng, shape, shards, -0.22, 0.18) if shards else 1.0
    entries = jax.random.normal(rng, shape, jnp.float32) * scale * level
    return jnp.minimum(jnp.maximum(entries, -bound), bound).astype(kind)


def setup_inputs(seed: int = 0, part: int = 0) -> dict:
    seeds = jax.random.split(jax.random.key(seed), 6)
    part_splits = jax.random.split(jax.random.fold_in(seeds[5], part), 6)
    intensity = gaussian(part_splits[0], (P_SIZE, NSAMP), 1.0, 6.0, ((0, 4), (1, 4)), jnp.float32)
    image_grad = gaussian(part_splits[1], (3, P_SIZE, NSAMP), 1.0, 6.0, ((1, 4), (2, 4)))
    owner_keys = jax.random.split(jax.random.fold_in(part_splits[2], 1), NSAMP // S_DEV)
    owner_turns = jax.random.permutation(jax.random.fold_in(part_splits[2], 3), NSAMP // S_DEV)
    owner = jax.vmap(lambda own, number: routed_block(jax.random.fold_in(part_splits[2], 2), own, number, S_DEV, N_SPACE, 1, CAP, 2))(owner_keys, owner_turns).reshape((NSAMP, 1))
    coord_xy = set_ends(jax.random.randint(part_splits[3], (2, NSAMP), 0, (GX - 3) * SPC), jax.random.fold_in(part_splits[3], 1), 0, ((GX - 3) * SPC) - 1).astype(jnp.int32)
    coord_z = set_ends(jax.random.randint(part_splits[4], (NSAMP,), 0, GZ_DEV * SPC), jax.random.fold_in(part_splits[4], 1), 0, (GZ_DEV * SPC) - 1).astype(jnp.int32)
    return dict(intensity=intensity, image_grad=image_grad, owner=owner, coord_xy=coord_xy, coord_z=coord_z)


def spline_values(offset):
    square = offset * offset
    cube = square * offset
    remain = 1.0 - offset
    return (remain * remain * remain / 6.0, (3.0 * cube - 6.0 * square + 4.0) / 6.0, (-3.0 * cube + 3.0 * square + 3.0 * offset + 1.0) / 6.0, cube / 6.0)

def reference(intensity, image_grad, owner, coord_xy, coord_z):
    samples = intensity.shape[1]
    phase_mean = lax.optimization_barrier(jnp.mean(intensity, axis=0))
    centered = intensity - phase_mean
    phase_var = lax.optimization_barrier(jnp.mean(centered * centered, axis=0))
    deviation = 2.0 * centered / jnp.sqrt(phase_var + 1.0)
    forces = (deviation[None] * image_grad.astype(jnp.float32)).reshape(3 * P_SIZE, samples)
    pos_x = coord_xy[0].astype(jnp.float32) / SPC
    pos_y = coord_xy[1].astype(jnp.float32) / SPC
    pos_z = coord_z.astype(jnp.float32) / SPC
    floor_x = jnp.floor(pos_x)
    floor_y = jnp.floor(pos_y)
    floor_z = jnp.floor(pos_z)
    offset_x = pos_x - floor_x
    offset_y = pos_y - floor_y
    offset_z = pos_z - floor_z
    corner_x = floor_x.astype(jnp.int32)
    corner_y = floor_y.astype(jnp.int32)
    corner_z = owner[:, 0].astype(jnp.int32) * GZ_DEV + floor_z.astype(jnp.int32)
    block_rows = min(4096, samples)
    block_count = samples // block_rows
    cells = (NZC + 3) * GX * GX
    steps_four = jnp.arange(4, dtype=jnp.int32)

    def accumulate(block_id, grid):
        start = (block_id * block_rows).astype(jnp.int32)

        def pick(array):
            return lax.dynamic_slice_in_dim(array, start, block_rows, array.ndim - 1)
        vals_x = jnp.stack(spline_values(pick(offset_x)), axis=1)
        vals_y = jnp.stack(spline_values(pick(offset_y)), axis=1)
        vals_z = jnp.stack(spline_values(pick(offset_z)), axis=1)
        force_rows = pick(forces)
        lifted = force_rows[:, None, :] * vals_z.T[None, :, :]
        lifted = lax.optimization_barrier(lifted.astype(jnp.bfloat16)).astype(jnp.float32)
        plane = vals_x[:, :, None] * vals_y[:, None, :]
        plane = lax.optimization_barrier(plane.astype(jnp.bfloat16)).astype(jnp.float32)
        contrib = jnp.transpose(lifted, (2, 1, 0))[:, :, None, None, :] * plane[:, None, :, :, None]
        rows_z = pick(corner_z)[:, None] + steps_four[None, :]
        rows_x = pick(corner_x)[:, None] + steps_four[None, :]
        rows_y = pick(corner_y)[:, None] + steps_four[None, :]
        index = (rows_z[:, :, None, None] * GX + rows_x[:, None, :, None]) * GX + rows_y[:, None, None, :]
        return grid.at[index.reshape(-1)].add(contrib.reshape(-1, 3 * P_SIZE))
    grid = lax.fori_loop(0, block_count, accumulate, jnp.zeros((cells, 3 * P_SIZE), jnp.float32))
    kept = grid[:NZC * GX * GX].reshape(NZC, GX * GX, 3, P_SIZE)
    return jnp.transpose(kept, (2, 3, 0, 1))
```

```python
import functools

import jax
import jax.numpy as jnp
from jax import lax
from jax.experimental import pallas as pl
from jax.experimental.pallas import tpu as pltpu
from jax.sharding import PartitionSpec as P

GX = 32
SPC = 16
GZ_DEV = 8
PIECES = 1
K_BLOCK = 1024
SUB = 256


def stats_kernel(intensity_ref, out_ref):
    values = intensity_ref[...]
    mean = jnp.mean(values, axis=0, keepdims=True)
    centered = values - mean
    out_ref[0:1] = mean
    out_ref[1:2] = jnp.sum(centered * centered, axis=0, keepdims=True)


def spline_weights(position, extent, first):
    shape = (extent, position.shape[1])
    index = lax.broadcasted_iota(jnp.int32, shape, 0) + first
    away = jnp.abs(index.astype(jnp.float32) - (position + 1.0))
    wide = jnp.maximum(2.0 - away, 0.0)
    near = jnp.maximum(1.0 - away, 0.0)
    return (wide * wide * wide - 4.0 * (near * near * near)) * (1.0 / 6.0)


def grid_kernel(
    intensity_ref, grad_ref, stats_ref, owner_ref, xy_ref, z_ref, out_ref,
    lifted_a, lifted_b, plane_a, plane_b,
    *, planes, phases, first_x, width_x,
):
    ph_dev, samples = intensity_ref.shape
    blocks = samples // K_BLOCK

    def build(block, lifted, plane):
        for sub in range(K_BLOCK // SUB):
            here = pl.ds(pl.multiple_of(block * K_BLOCK + sub * SUB, SUB), SUB)
            cols = slice(sub * SUB, (sub + 1) * SUB)
            mean = stats_ref[0:1, here]
            var = stats_ref[1:2, here] * (1.0 / phases)
            scale = 2.0 / jnp.sqrt(var + 1.0)
            deviation = (intensity_ref[:, here] - mean) * scale
            pos_x = xy_ref[0:1, here].astype(jnp.float32) * (1.0 / SPC)
            pos_y = xy_ref[1:2, here].astype(jnp.float32) * (1.0 / SPC)
            pos_z = z_ref[0:1, here].astype(jnp.float32) * (1.0 / SPC)
            pos_z = pos_z + (owner_ref[0:1, here] * GZ_DEV).astype(jnp.float32)
            along_z = spline_weights(pos_z, planes, 0)
            for c in range(3):
                force = deviation * grad_ref[c, :, here].astype(jnp.float32)
                for p in range(ph_dev):
                    row = (c * ph_dev + p) * planes
                    lifted[row:row + planes, cols] = (force[p:p + 1] * along_z).astype(jnp.bfloat16)
            along_y = spline_weights(pos_y, GX, 0)
            along_x = spline_weights(pos_x, width_x, first_x)
            for x in range(width_x):
                plane[x * GX:(x + 1) * GX, cols] = (along_x[x:x + 1] * along_y).astype(jnp.bfloat16)

    def multiply(lifted, plane):
        return lax.dot_general(
            lifted[...], plane[...], (((1,), (1,)), ((), ())),
            preferred_element_type=jnp.float32)

    out_ref[...] = jnp.zeros(out_ref.shape, jnp.float32)
    build(0, lifted_a, plane_a)

    def pair(i, carry):
        build(2 * i + 1, lifted_b, plane_b)
        out_ref[...] += multiply(lifted_a, plane_a)
        build(jnp.minimum(2 * i + 2, blocks - 1), lifted_a, plane_a)
        out_ref[...] += multiply(lifted_b, plane_b)
        return carry

    lax.fori_loop(0, blocks // 2, pair, 0)


def partial_grid(intensity, image_grad, stats, owner, coord_xy, coord_z, planes, phases, piece, pieces):
    ph_dev = intensity.shape[0]
    width_x = GX // pieces
    rows = 3 * ph_dev * planes
    return pl.pallas_call(
        functools.partial(grid_kernel, planes=planes, phases=phases,
                          first_x=piece * width_x, width_x=width_x),
        out_shape=jax.ShapeDtypeStruct((rows, width_x * GX), jnp.float32),
        scratch_shapes=[
            pltpu.VMEM((rows, K_BLOCK), jnp.bfloat16),
            pltpu.VMEM((rows, K_BLOCK), jnp.bfloat16),
            pltpu.VMEM((width_x * GX, K_BLOCK), jnp.bfloat16),
            pltpu.VMEM((width_x * GX, K_BLOCK), jnp.bfloat16),
        ],
        compiler_params=pltpu.CompilerParams(vmem_limit_bytes=56 << 20),
    )(intensity, image_grad, stats, owner, coord_xy, coord_z).reshape(3 * ph_dev, planes, width_x * GX)


def phase_stats(intensity):
    ph_dev, samples = intensity.shape
    size = lax.axis_size("phase")
    stats = pl.pallas_call(
        stats_kernel, out_shape=jax.ShapeDtypeStruct((2, samples), jnp.float32))(intensity)
    count = float(ph_dev)
    step = 1
    while step < size:
        other = lax.ppermute(stats, "phase", [(i, i ^ step) for i in range(size)])
        gap = other[0] - stats[0]
        stats = jnp.stack([
            0.5 * (stats[0] + other[0]),
            stats[1] + other[1] + gap * gap * (0.5 * count)])
        count *= 2.0
        step *= 2
    return stats


def scatter_planes(partial):
    size = lax.axis_size("space")
    me = lax.axis_index("space")

    def own(target):
        return lax.dynamic_slice_in_dim(
            partial, jnp.clip(target, 0, size - 1) * GZ_DEV, GZ_DEV, 1)

    up = own(size - 1)
    down = own(0)
    for step in range(1, size):
        if step > 1:
            up = up + own(size + me - step)
            down = down + own(me + step - size)
        up = lax.ppermute(up, "space", [(i, i + 1) for i in range(min(step, size - 1))])
        down = lax.ppermute(down, "space", [(size - 1 - i, size - 2 - i) for i in range(min(step, size - 1))])
    return own(me) + up + down


def local(intensity, image_grad, owner, coord_xy, coord_z):
    ph_dev, samples = intensity.shape
    planes = lax.axis_size("space") * GZ_DEV
    phases = ph_dev * lax.axis_size("phase")
    stats = phase_stats(intensity)
    owner = owner.reshape(1, samples)
    coord_z = coord_z.reshape(1, samples)
    partial = partial_grid(intensity, image_grad, stats, owner, coord_xy, coord_z, planes, phases, 0, 1)
    mine = scatter_planes(partial)
    return mine.reshape(3, ph_dev, GZ_DEV, GX * GX)


def solution(mesh):
    return jax.shard_map(
        local,
        mesh=mesh,
        in_specs=(
            P("phase", ("groups", "space")),
            P(None, "phase", ("groups", "space")),
            P(("groups", "space"), None),
            P(None, ("groups", "space")),
            P(("groups", "space")),
        ),
        out_specs=P("groups", "phase", "space", None),
        check_vma=False,
    )
```

```python
import functools

import jax
import jax.numpy as jnp
from jax import lax
from jax.experimental import pallas as pl
from jax.experimental.pallas import tpu as pltpu
from jax.sharding import PartitionSpec as P


GX = 32
SPC = 16
GZ_DEV = 8
K_BLOCK = 2048
SUB = 512
STEP = 512
SPLIT = (16, 16)
COST = pl.CostEstimate(flops=1 << 30, bytes_accessed=12 << 20, transcendentals=0)

IN_VMEM = pl.BlockSpec(memory_space=pltpu.VMEM)


def spline_weights(position, extent, first):
    shape = (extent, position.shape[1])
    index = lax.broadcasted_iota(jnp.int32, shape, 0) + first
    away = jnp.abs(index.astype(jnp.float32) - (position + 1.0))
    wide = jnp.maximum(2.0 - away, 0.0)
    near = jnp.maximum(1.0 - away, 0.0)
    return (wide * wide * wide - 4.0 * (near * near * near)) * (1.0 / 6.0)


def stats_kernel(intensity_ref, out_ref):
    values = intensity_ref[...]
    mean = jnp.mean(values, axis=0, keepdims=True)
    centered = values - mean
    out_ref[0:1] = mean
    out_ref[1:2] = jnp.sum(centered * centered, axis=0, keepdims=True)


def phase_stats(intensity):
    return pl.pallas_call(
        stats_kernel,
        out_shape=jax.ShapeDtypeStruct((2, intensity.shape[1]), jnp.float32),
        compiler_params=pltpu.CompilerParams(vmem_limit_bytes=4 << 20),
        cost_estimate=COST,
        name="phase_stats",
    )(intensity)


def weights_kernel(coord_ref, x_ref, y_ref):
    def step(i, carry):
        here = pl.ds(pl.multiple_of(i * STEP, STEP), STEP)
        for row, out_ref in enumerate((x_ref, y_ref)):
            position = coord_ref[row:row + 1, here].astype(jnp.float32) * (1.0 / SPC)
            out_ref[:, here] = spline_weights(position, GX, 0)
        return carry

    lax.fori_loop(0, coord_ref.shape[1] // STEP, step, 0)


def plane_weights(coord_xy):
    samples = coord_xy.shape[1]
    return pl.pallas_call(
        weights_kernel,
        out_shape=[jax.ShapeDtypeStruct((GX, samples), jnp.float32)] * 2,
        in_specs=[IN_VMEM],
        out_specs=[IN_VMEM, IN_VMEM],
        compiler_params=pltpu.CompilerParams(vmem_limit_bytes=4 << 20),
        cost_estimate=COST,
        name="plane_weights",
    )(coord_xy)


def forces_at(here, intensity_ref, grad_ref, stats_refs):
    ph_dev = intensity_ref.shape[0]
    means = [ref[0:1, here] for ref in stats_refs]
    mean = sum(means) * (1.0 / len(means))
    spread = sum(ref[1:2, here] for ref in stats_refs)
    spread = spread + sum((m - mean) * (m - mean) for m in means) * float(ph_dev)
    var = spread * (1.0 / (ph_dev * len(means)))
    deviation = (intensity_ref[:, here] - mean) * (2.0 / jnp.sqrt(var + 1.0))
    return [deviation * grad_ref[c, :, here].astype(jnp.float32) for c in range(3)]


def pair_kernel(*refs, n_stats, owners, first_x):
    *refs, lifted_a, lifted_b, plane_a, plane_b, total = refs
    if n_stats:
        intensity_ref, grad_ref, owner_ref, z_ref = refs[:4]
        stats_refs = refs[4:4 + n_stats]
        x_ref, y_ref, _, first_ref, second_ref, force_ref, height_ref = refs[4 + n_stats:]
    else:
        force_ref, height_ref, x_ref, y_ref, _, first_ref, second_ref = refs
    rows, samples = force_ref.shape
    half = rows * GZ_DEV
    blocks = samples // K_BLOCK
    firsts = [jnp.asarray(one * GZ_DEV, jnp.int32).astype(jnp.float32) for one in owners()]

    def prepare(here):
        ph_dev = rows // 3
        pos_z = z_ref[0:1, here].astype(jnp.float32) * (1.0 / SPC)
        height_ref[0:1, here] = pos_z + (owner_ref[0:1, here] * GZ_DEV).astype(jnp.float32)
        for c, force in enumerate(forces_at(here, intensity_ref, grad_ref, stats_refs)):
            force_ref[c * ph_dev:(c + 1) * ph_dev, here] = force

    def build(block, lifted, plane):
        for sub in range(K_BLOCK // SUB):
            here = pl.ds(pl.multiple_of(block * K_BLOCK + sub * SUB, SUB), SUB)
            cols = slice(sub * SUB, (sub + 1) * SUB)
            if n_stats:
                prepare(here)
            height = height_ref[0:1, here]
            for o, first_plane in enumerate(firsts):
                along_z = spline_weights(height - first_plane, GZ_DEV, 0)
                for r in range(0, rows, 2):
                    two = [force_ref[q:q + 1, here] * along_z for q in (r, r + 1)]
                    row = o * half + r * GZ_DEV
                    lifted[row:row + 2 * GZ_DEV, cols] = jnp.concatenate(two, axis=0).astype(jnp.bfloat16)
            along_y = y_ref[:, here]
            for x in range(plane.shape[0] // GX):
                along_x = x_ref[first_x + x:first_x + x + 1, here]
                plane[x * GX:(x + 1) * GX, cols] = (along_x * along_y).astype(jnp.bfloat16)

    def multiply(lifted, plane):
        return lax.dot_general(
            plane[...], lifted[...], (((1,), (1,)), ((), ())), preferred_element_type=jnp.float32)

    build(0, lifted_a, plane_a)
    total[...] = jnp.zeros(total.shape, jnp.float32)

    def pair(i, carry):
        build(2 * i + 1, lifted_b, plane_b)
        total[...] += multiply(lifted_a, plane_a)
        build(jnp.minimum(2 * i + 2, blocks - 1), lifted_a, plane_a)
        total[...] += multiply(lifted_b, plane_b)
        return carry

    lax.fori_loop(0, blocks // 2, pair, 0)
    both = total[...].T
    first_ref[...] = both[:half]
    second_ref[...] = both[half:]


def pair_grid(owners, args, first_x, width, after, stats=()):
    if stats:
        rows, samples = 3 * args[0].shape[0], args[0].shape[1]
    else:
        rows, samples = args[0].shape
    half = rows * GZ_DEV
    cells = width * GX
    out_shape = [jax.ShapeDtypeStruct((half, cells), jnp.float32)] * 2
    if stats:
        out_shape += [jax.ShapeDtypeStruct((rows, samples), jnp.float32),
                      jax.ShapeDtypeStruct((1, samples), jnp.float32)]
    outs = pl.pallas_call(
        functools.partial(pair_kernel, n_stats=len(stats), owners=owners, first_x=first_x),
        out_shape=out_shape,
        in_specs=[IN_VMEM for _ in args] + [pl.BlockSpec(memory_space=pl.ANY)],
        out_specs=[IN_VMEM for _ in out_shape],
        scratch_shapes=[
            pltpu.VMEM((2 * half, K_BLOCK), jnp.bfloat16),
            pltpu.VMEM((2 * half, K_BLOCK), jnp.bfloat16),
            pltpu.VMEM((cells, K_BLOCK), jnp.bfloat16),
            pltpu.VMEM((cells, K_BLOCK), jnp.bfloat16),
            pltpu.VMEM((cells, 2 * half), jnp.float32),
        ],
        compiler_params=pltpu.CompilerParams(vmem_limit_bytes=24 << 20),
        cost_estimate=COST,
        name="pair_grid",
    )(*args, after)
    return [o.reshape(rows, GZ_DEV, cells) for o in outs[:2]], outs[2:]


def from_other_phases(stats):
    size = lax.axis_size("phase")
    return [
        lax.ppermute(stats, "phase", [(i, (i + k) % size) for i in range(size)])
        for k in range(1, size)]


def chain(chunk_of):
    size = lax.axis_size("space")
    me = lax.axis_index("space")
    up = down = None
    for step in range(1, size):
        send_up, send_down = chunk_of(size + me - step), chunk_of(me + step - size)
        up = send_up if up is None else up + send_up
        down = send_down if down is None else down + send_down
        up = lax.ppermute(up, "space", [(i, i + 1) for i in range(step)])
        down = lax.ppermute(down, "space", [(size - 1 - i, size - 2 - i) for i in range(step)])
    total = chunk_of(me)
    return total if up is None else total + up + down


FIRST = [(0, 1), (1, 3), (3, 2), (2, 0)]
SIDE = [(0, 1), (1, 0), (2, 3), (3, 2)]
ACROSS = [(0, 3), (3, 0), (1, 2), (2, 1)]


def flipped(first, second):
    def owners():
        me = lax.axis_index("space")
        return me ^ first, me ^ second

    return owners


def inner_device():
    me = lax.axis_index("space")
    return (me == 1) | (me == 2)


def join_kernel(own_ref, got_ref, out_ref):
    out_ref[...] = own_ref[...] + jnp.where(inner_device(), got_ref[...], 0.0)


def finish_kernel(*refs):
    out_ref = refs[-1]
    start = 0
    for piece in range((len(refs) - 1) // 4):
        mine, side, first, across = refs[4 * piece:4 * piece + 4]
        cells = mine.shape[-1]
        out_ref[:, :, start:start + cells] = (
            mine[...] + side[...] + across[...] + jnp.where(inner_device(), 0.0, first[...]))
        start += cells


def in_vmem(kernel, shape, args, out_spec):
    return pl.pallas_call(
        kernel, out_shape=jax.ShapeDtypeStruct(shape, jnp.float32),
        in_specs=[IN_VMEM for _ in args], out_specs=out_spec,
        compiler_params=pltpu.CompilerParams(vmem_limit_bytes=8 << 20))(*args)


def four_owners(pair_of, pieces):
    firsts, acrosses, threes, args = [], [], [], []

    def relay(piece):
        joined = in_vmem(join_kernel, threes[piece].shape, (threes[piece], firsts[piece]), IN_VMEM)
        acrosses.append(lax.ppermute(joined, "space", ACROSS))
        return joined

    after = None
    for piece in range(pieces):
        two, three = pair_of(flipped(2, 3), piece, after)
        firsts.append(lax.ppermute(two, "space", FIRST))
        threes.append(three)
        after = two
    for piece in range(pieces):
        after = relay(piece)
        one, mine = pair_of(flipped(1, 0), piece, after)
        args += [mine, lax.ppermute(one, "space", SIDE), firsts[piece], acrosses[piece]]
    shape = mine.shape[:2] + (sum(a.shape[-1] for a in args[::4]),)
    return in_vmem(finish_kernel, shape, args, pl.BlockSpec())


def local(intensity, image_grad, owner, coord_xy, coord_z):
    ph_dev, samples = intensity.shape
    size = lax.axis_size("space")
    stats = phase_stats(intensity)
    stats = [stats] + from_other_phases(stats)
    weights = plane_weights(coord_xy)
    raw = [intensity, image_grad, owner.reshape(1, samples), coord_z.reshape(1, samples)]
    prepared = []

    def pair_of(owners, piece, after=None):
        first_x, width = sum(SPLIT[:piece]), SPLIT[piece]
        after = stats[0] if after is None else after
        if prepared:
            return pair_grid(owners, [*prepared, *weights], first_x, width, after)[0]
        outs, kept = pair_grid(owners, [*raw, *stats, *weights], first_x, width, after, stats=stats)
        prepared.extend(kept)
        return outs

    if size == 4:
        grid = four_owners(pair_of, len(SPLIT))
    else:
        columns = []
        for piece in range(len(SPLIT)):
            chunks = []
            for start in range(0, size, 2):
                chunks += pair_of(lambda start=start: (start, min(start + 1, size - 1)), piece)
            table = jnp.stack(chunks)
            columns.append(chain(lambda j: lax.dynamic_index_in_dim(
                table, jnp.clip(j, 0, size - 1), 0, keepdims=False)))
        grid = jnp.concatenate(columns, axis=-1)
    return grid.reshape(3, ph_dev, GZ_DEV, GX * GX)


def solution(mesh):
    return jax.shard_map(
        local,
        mesh=mesh,
        in_specs=(
            P("phase", ("groups", "space")),
            P(None, "phase", ("groups", "space")),
            P(("groups", "space"), None),
            P(None, ("groups", "space")),
            P(("groups", "space")),
        ),
        out_specs=P("groups", "phase", "space", None),
        check_vma=False,
    )
```

```python
import functools

import jax
import jax.numpy as jnp
from jax import lax
from jax.experimental import pallas as pl
from jax.experimental.pallas import tpu as pltpu
from jax.sharding import PartitionSpec as P


GX = 32
SPC = 16
GZ_DEV = 8
BLOCKS = (1024, 2048, 4096, 4608)
SUB = 512
STEP = 512
SPLIT = (16, 16)
NEAR_SPLIT = (20, 12)
COST = pl.CostEstimate(flops=1 << 30, bytes_accessed=12 << 20, transcendentals=0)

IN_VMEM = pl.BlockSpec(memory_space=pltpu.VMEM)


def spline_weights(position, extent, first):
    shape = (extent, position.shape[1])
    index = lax.broadcasted_iota(jnp.int32, shape, 0) + first
    away = jnp.abs(index.astype(jnp.float32) - (position + 1.0))
    wide = jnp.maximum(2.0 - away, 0.0)
    near = jnp.maximum(1.0 - away, 0.0)
    return (wide * wide * wide - 4.0 * (near * near * near)) * (1.0 / 6.0)


def stats_kernel(intensity_ref, out_ref):
    values = intensity_ref[...]
    mean = jnp.mean(values, axis=0, keepdims=True)
    centered = values - mean
    out_ref[0:1] = mean
    out_ref[1:2] = jnp.sum(centered * centered, axis=0, keepdims=True)


def phase_stats(intensity):
    return pl.pallas_call(
        stats_kernel,
        out_shape=jax.ShapeDtypeStruct((2, intensity.shape[1]), jnp.float32),
        compiler_params=pltpu.CompilerParams(vmem_limit_bytes=4 << 20),
        cost_estimate=COST,
        name="phase_stats",
    )(intensity)


def weights_kernel(coord_ref, x_ref, y_ref):
    def step(i, carry):
        here = pl.ds(pl.multiple_of(i * STEP, STEP), STEP)
        for row, out_ref in enumerate((x_ref, y_ref)):
            position = coord_ref[row:row + 1, here].astype(jnp.float32) * (1.0 / SPC)
            out_ref[:, here] = spline_weights(position, GX, 0)
        return carry

    lax.fori_loop(0, coord_ref.shape[1] // STEP, step, 0)


def plane_weights(coord_xy):
    samples = coord_xy.shape[1]
    return pl.pallas_call(
        weights_kernel,
        out_shape=[jax.ShapeDtypeStruct((GX, samples), jnp.float32)] * 2,
        in_specs=[IN_VMEM],
        out_specs=[IN_VMEM, IN_VMEM],
        compiler_params=pltpu.CompilerParams(vmem_limit_bytes=4 << 20),
        cost_estimate=COST,
        name="plane_weights",
    )(coord_xy)


def forces_at(here, intensity_ref, grad_ref, stats_refs):
    ph_dev = intensity_ref.shape[0]
    means = [ref[0:1, here] for ref in stats_refs]
    mean = sum(means) * (1.0 / len(means))
    spread = sum(ref[1:2, here] for ref in stats_refs)
    spread = spread + sum((m - mean) * (m - mean) for m in means) * float(ph_dev)
    var = spread * (1.0 / (ph_dev * len(means)))
    deviation = (intensity_ref[:, here] - mean) * (2.0 / jnp.sqrt(var + 1.0))
    return [deviation * grad_ref[c, :, here].astype(jnp.float32) for c in range(3)]


def block_sizes(samples):
    sizes, left = [], samples
    for size in BLOCKS:
        sizes.append(min(size, left))
        left -= sizes[-1]
    while left:
        sizes.append(min(BLOCKS[-1], left))
        left -= sizes[-1]
    return [size for size in sizes if size]


def pair_kernel(*refs, n_stats, owners, first_x):
    *refs, lifted_a, lifted_b, plane_a, plane_b, total = refs
    if n_stats:
        intensity_ref, grad_ref, owner_ref, z_ref = refs[:4]
        stats_refs = refs[4:4 + n_stats]
        x_ref, y_ref, _, first_ref, second_ref, force_ref, height_ref = refs[4 + n_stats:]
    else:
        force_ref, height_ref, x_ref, y_ref, _, first_ref, second_ref = refs
    rows, samples = force_ref.shape
    half = rows * GZ_DEV
    sizes = block_sizes(samples)
    begins = [sum(sizes[:i]) for i in range(len(sizes))]
    firsts = [jnp.asarray(one * GZ_DEV, jnp.int32).astype(jnp.float32) for one in owners()]

    def prepare(here):
        ph_dev = rows // 3
        pos_z = z_ref[0:1, here].astype(jnp.float32) * (1.0 / SPC)
        height_ref[0:1, here] = pos_z + (owner_ref[0:1, here] * GZ_DEV).astype(jnp.float32)
        for c, force in enumerate(forces_at(here, intensity_ref, grad_ref, stats_refs)):
            force_ref[c * ph_dev:(c + 1) * ph_dev, here] = force

    def build(block, lifted, plane):
        for sub in range(sizes[block] // SUB):
            here = pl.ds(begins[block] + sub * SUB, SUB)
            cols = slice(sub * SUB, (sub + 1) * SUB)
            if n_stats:
                prepare(here)
            height = height_ref[0:1, here]
            for o, first_plane in enumerate(firsts):
                along_z = spline_weights(height - first_plane, GZ_DEV, 0)
                for r in range(0, rows, 2):
                    two = [force_ref[q:q + 1, here] * along_z for q in (r, r + 1)]
                    row = o * half + r * GZ_DEV
                    lifted[row:row + 2 * GZ_DEV, cols] = jnp.concatenate(two, axis=0).astype(jnp.bfloat16)
            along_y = y_ref[:, here]
            for x in range(plane.shape[0] // GX):
                along_x = x_ref[first_x + x:first_x + x + 1, here]
                plane[x * GX:(x + 1) * GX, cols] = (along_x * along_y).astype(jnp.bfloat16)

    def multiply(block, lifted, plane):
        size = sizes[block]
        return lax.dot_general(
            plane[:, :size], lifted[:, :size], (((1,), (1,)), ((), ())),
            preferred_element_type=jnp.float32)

    buffers = ((lifted_a, plane_a), (lifted_b, plane_b))
    build(0, *buffers[0])
    for block in range(len(sizes)):
        if block + 1 < len(sizes):
            build(block + 1, *buffers[(block + 1) % 2])
        part = multiply(block, *buffers[block % 2])
        if block:
            total[...] += part
        else:
            total[...] = part
    both = total[...].T
    first_ref[...] = both[:half]
    second_ref[...] = both[half:]


def pair_grid(owners, args, first_x, width, after, stats=()):
    if stats:
        rows, samples = 3 * args[0].shape[0], args[0].shape[1]
    else:
        rows, samples = args[0].shape
    half = rows * GZ_DEV
    cells = width * GX
    largest = max(block_sizes(samples))
    out_shape = [jax.ShapeDtypeStruct((half, cells), jnp.float32)] * 2
    if stats:
        out_shape += [jax.ShapeDtypeStruct((rows, samples), jnp.float32),
                      jax.ShapeDtypeStruct((1, samples), jnp.float32)]
    outs = pl.pallas_call(
        functools.partial(pair_kernel, n_stats=len(stats), owners=owners, first_x=first_x),
        out_shape=out_shape,
        in_specs=[IN_VMEM for _ in args] + [pl.BlockSpec(memory_space=pl.ANY)],
        out_specs=[IN_VMEM for _ in out_shape],
        scratch_shapes=[
            pltpu.VMEM((2 * half, largest), jnp.bfloat16),
            pltpu.VMEM((2 * half, largest), jnp.bfloat16),
            pltpu.VMEM((cells, largest), jnp.bfloat16),
            pltpu.VMEM((cells, largest), jnp.bfloat16),
            pltpu.VMEM((cells, 2 * half), jnp.float32),
        ],
        compiler_params=pltpu.CompilerParams(vmem_limit_bytes=24 << 20),
        cost_estimate=COST,
        name="pair_grid",
    )(*args, after)
    return [o.reshape(rows, GZ_DEV, cells) for o in outs[:2]], outs[2:]


def from_other_phases(stats):
    size = lax.axis_size("phase")
    if size == 4:
        chip = lax.ppermute(stats, "phase", [(i, i ^ 2) for i in range(size)])
        core = lax.ppermute(stats, "phase", [(i, i ^ 1) for i in range(size)])
        return [core, chip, lax.ppermute(chip, "phase", [(i, i ^ 1) for i in range(size)])]
    return [
        lax.ppermute(stats, "phase", [(i, (i + k) % size) for i in range(size)])
        for k in range(1, size)]


def chain(chunk_of):
    size = lax.axis_size("space")
    me = lax.axis_index("space")
    up = down = None
    for step in range(1, size):
        send_up, send_down = chunk_of(size + me - step), chunk_of(me + step - size)
        up = send_up if up is None else up + send_up
        down = send_down if down is None else down + send_down
        up = lax.ppermute(up, "space", [(i, i + 1) for i in range(step)])
        down = lax.ppermute(down, "space", [(size - 1 - i, size - 2 - i) for i in range(step)])
    total = chunk_of(me)
    return total if up is None else total + up + down


FIRST = [(0, 1), (1, 3), (3, 2), (2, 0)]
SIDE = [(0, 1), (1, 0), (2, 3), (3, 2)]
ACROSS = [(0, 3), (3, 0), (1, 2), (2, 1)]


def flipped(first, second):
    def owners():
        me = lax.axis_index("space")
        return me ^ first, me ^ second

    return owners


def inner_device():
    me = lax.axis_index("space")
    return (me == 1) | (me == 2)


def join_kernel(own_ref, got_ref, out_ref):
    out_ref[...] = own_ref[...] + jnp.where(inner_device(), got_ref[...], 0.0)


def finish_kernel(*refs):
    out_ref = refs[-1]
    start = 0
    for piece in range(len(NEAR_SPLIT)):
        mine, side = refs[2 * piece:2 * piece + 2]
        cells = mine.shape[-1]
        out_ref[:, :, start:start + cells] = mine[...] + side[...]
        start += cells
    refs = refs[2 * len(NEAR_SPLIT):-1]
    start = 0
    for piece in range(len(SPLIT)):
        first, across = refs[2 * piece:2 * piece + 2]
        cells = first.shape[-1]
        out_ref[:, :, start:start + cells] += across[...] + jnp.where(inner_device(), 0.0, first[...])
        start += cells


def in_vmem(kernel, shape, args, out_spec):
    return pl.pallas_call(
        kernel, out_shape=jax.ShapeDtypeStruct(shape, jnp.float32),
        in_specs=[IN_VMEM for _ in args], out_specs=out_spec,
        compiler_params=pltpu.CompilerParams(vmem_limit_bytes=8 << 20))(*args)


def four_owners(pair_of):
    far, near = [], []
    threes, after = [], None
    for piece in range(len(SPLIT)):
        two, three = pair_of(flipped(2, 3), SPLIT, piece, after)
        far.append([lax.ppermute(two, "space", FIRST)])
        threes.append(three)
        after = two
    for piece in range(len(NEAR_SPLIT)):
        if piece < len(SPLIT):
            after = in_vmem(join_kernel, threes[piece].shape, (threes[piece], *far[piece]), IN_VMEM)
            far[piece].append(lax.ppermute(after, "space", ACROSS))
        one, mine = pair_of(flipped(1, 0), NEAR_SPLIT, piece, after)
        near.append([mine, lax.ppermute(one, "space", SIDE)])
    args = [a for pair in near + far for a in pair]
    return in_vmem(finish_kernel, mine.shape[:2] + (GX * GX,), args, pl.BlockSpec())


def local(intensity, image_grad, owner, coord_xy, coord_z):
    ph_dev, samples = intensity.shape
    size = lax.axis_size("space")
    stats = phase_stats(intensity)
    stats = [stats] + from_other_phases(stats)
    weights = plane_weights(coord_xy)
    raw = [intensity, image_grad, owner.reshape(1, samples), coord_z.reshape(1, samples)]
    prepared = []

    def pair_of(owners, split, piece, after=None):
        first_x, width = sum(split[:piece]), split[piece]
        after = stats[0] if after is None else after
        if prepared:
            return pair_grid(owners, [*prepared, *weights], first_x, width, after)[0]
        outs, kept = pair_grid(owners, [*raw, *stats, *weights], first_x, width, after, stats=stats)
        prepared.extend(kept)
        return outs

    if size == 4:
        grid = four_owners(pair_of)
    else:
        columns = []
        for piece in range(len(SPLIT)):
            chunks = []
            for start in range(0, size, 2):
                chunks += pair_of(lambda start=start: (start, min(start + 1, size - 1)), SPLIT, piece)
            table = jnp.stack(chunks)
            columns.append(chain(lambda j: lax.dynamic_index_in_dim(
                table, jnp.clip(j, 0, size - 1), 0, keepdims=False)))
        grid = jnp.concatenate(columns, axis=-1)
    return grid.reshape(3, ph_dev, GZ_DEV, GX * GX)


def solution(mesh):
    return jax.shard_map(
        local,
        mesh=mesh,
        in_specs=(
            P("phase", ("groups", "space")),
            P(None, "phase", ("groups", "space")),
            P(("groups", "space"), None),
            P(None, ("groups", "space")),
            P(("groups", "space")),
        ),
        out_specs=P("groups", "phase", "space", None),
        check_vma=False,
    )
```

```python
import functools

import jax
import jax.numpy as jnp
from jax import lax
from jax.experimental import pallas as pl
from jax.experimental.pallas import tpu as pltpu
from jax.sharding import PartitionSpec as P


GX = 32
SPC = 16
GZ_DEV = 8
BLOCKS = (1536, 3072, 5632, 6144)
SUB = 512
STEP = 512
SPLIT = (16, 16)
NEAR_SPLIT = (16, 16)
COST = pl.CostEstimate(flops=1 << 30, bytes_accessed=12 << 20, transcendentals=0)

IN_VMEM = pl.BlockSpec(memory_space=pltpu.VMEM)


def spline_weights(position, extent, first):
    shape = (extent, position.shape[1])
    index = lax.broadcasted_iota(jnp.int32, shape, 0) + first
    away = jnp.abs(index.astype(jnp.float32) - (position + 1.0))
    wide = jnp.maximum(2.0 - away, 0.0)
    near = jnp.maximum(1.0 - away, 0.0)
    return (wide * wide * wide - 4.0 * (near * near * near)) * (1.0 / 6.0)


def stats_kernel(intensity_ref, out_ref):
    values = intensity_ref[...]
    mean = jnp.mean(values, axis=0, keepdims=True)
    centered = values - mean
    out_ref[0:1] = mean
    out_ref[1:2] = jnp.sum(centered * centered, axis=0, keepdims=True)


def phase_stats(intensity):
    return pl.pallas_call(
        stats_kernel,
        out_shape=jax.ShapeDtypeStruct((2, intensity.shape[1]), jnp.float32),
        compiler_params=pltpu.CompilerParams(vmem_limit_bytes=4 << 20),
        cost_estimate=COST,
        name="phase_stats",
    )(intensity)


def weights_kernel(coord_ref, x_ref, y_ref):
    def step(i, carry):
        here = pl.ds(pl.multiple_of(i * STEP, STEP), STEP)
        for row, out_ref in enumerate((x_ref, y_ref)):
            position = coord_ref[row:row + 1, here].astype(jnp.float32) * (1.0 / SPC)
            out_ref[:, here] = spline_weights(position, GX, 0)
        return carry

    lax.fori_loop(0, coord_ref.shape[1] // STEP, step, 0)


def plane_weights(coord_xy):
    samples = coord_xy.shape[1]
    return pl.pallas_call(
        weights_kernel,
        out_shape=[jax.ShapeDtypeStruct((GX, samples), jnp.float32)] * 2,
        in_specs=[IN_VMEM],
        out_specs=[IN_VMEM, IN_VMEM],
        compiler_params=pltpu.CompilerParams(vmem_limit_bytes=4 << 20),
        cost_estimate=COST,
        name="plane_weights",
    )(coord_xy)


def forces_at(here, intensity_ref, grad_ref, stats_refs):
    ph_dev = intensity_ref.shape[0]
    means = [ref[0:1, here] for ref in stats_refs]
    mean = sum(means) * (1.0 / len(means))
    spread = sum(ref[1:2, here] for ref in stats_refs)
    spread = spread + sum((m - mean) * (m - mean) for m in means) * float(ph_dev)
    var = spread * (1.0 / (ph_dev * len(means)))
    deviation = (intensity_ref[:, here] - mean) * (2.0 / jnp.sqrt(var + 1.0))
    return [deviation * grad_ref[c, :, here].astype(jnp.float32) for c in range(3)]


def block_sizes(samples):
    sizes, left = [], samples
    for size in BLOCKS:
        sizes.append(min(size, left))
        left -= sizes[-1]
    while left:
        sizes.append(min(BLOCKS[-1], left))
        left -= sizes[-1]
    return [size for size in sizes if size]


def pair_kernel(*refs, n_stats, owners, first_x):
    *refs, lifted_a, lifted_b, plane_a, plane_b, total = refs
    if n_stats:
        intensity_ref, grad_ref, owner_ref, z_ref = refs[:4]
        stats_refs = refs[4:4 + n_stats]
        x_ref, y_ref, _, first_ref, second_ref, force_ref, height_ref = refs[4 + n_stats:]
    else:
        force_ref, height_ref, x_ref, y_ref, _, first_ref, second_ref = refs
    rows, samples = force_ref.shape
    half = rows * GZ_DEV
    sizes = block_sizes(samples)
    begins = [sum(sizes[:i]) for i in range(len(sizes))]
    firsts = [jnp.asarray(one * GZ_DEV, jnp.int32).astype(jnp.float32) for one in owners()]

    def prepare(here):
        ph_dev = rows // 3
        pos_z = z_ref[0:1, here].astype(jnp.float32) * (1.0 / SPC)
        height_ref[0:1, here] = pos_z + (owner_ref[0:1, here] * GZ_DEV).astype(jnp.float32)
        for c, force in enumerate(forces_at(here, intensity_ref, grad_ref, stats_refs)):
            force_ref[c * ph_dev:(c + 1) * ph_dev, here] = force

    def build(block, lifted, plane):
        for sub in range(sizes[block] // SUB):
            here = pl.ds(begins[block] + sub * SUB, SUB)
            cols = slice(sub * SUB, (sub + 1) * SUB)
            if n_stats:
                prepare(here)
            height = height_ref[0:1, here]
            for o, first_plane in enumerate(firsts):
                along_z = spline_weights(height - first_plane, GZ_DEV, 0)
                for r in range(0, rows, 2):
                    two = [force_ref[q:q + 1, here] * along_z for q in (r, r + 1)]
                    row = o * half + r * GZ_DEV
                    lifted[row:row + 2 * GZ_DEV, cols] = jnp.concatenate(two, axis=0).astype(jnp.bfloat16)
            along_y = y_ref[:, here]
            for x in range(plane.shape[0] // GX):
                along_x = x_ref[first_x + x:first_x + x + 1, here]
                plane[x * GX:(x + 1) * GX, cols] = (along_x * along_y).astype(jnp.bfloat16)

    def multiply(block, lifted, plane):
        size = sizes[block]
        return lax.dot_general(
            plane[:, :size], lifted[:, :size], (((1,), (1,)), ((), ())),
            preferred_element_type=jnp.float32)

    buffers = ((lifted_a, plane_a), (lifted_b, plane_b))
    build(0, *buffers[0])
    for block in range(len(sizes)):
        if block + 1 < len(sizes):
            build(block + 1, *buffers[(block + 1) % 2])
        part = multiply(block, *buffers[block % 2])
        if block:
            part = total[...] + part
        if block + 1 < len(sizes):
            total[...] = part
    both = part.T
    first_ref[...] = both[:half]
    second_ref[...] = both[half:]


def pair_grid(owners, args, first_x, width, after, stats=()):
    if stats:
        rows, samples = 3 * args[0].shape[0], args[0].shape[1]
    else:
        rows, samples = args[0].shape
    half = rows * GZ_DEV
    cells = width * GX
    largest = max(block_sizes(samples))
    out_shape = [jax.ShapeDtypeStruct((half, cells), jnp.float32)] * 2
    if stats:
        out_shape += [jax.ShapeDtypeStruct((rows, samples), jnp.float32),
                      jax.ShapeDtypeStruct((1, samples), jnp.float32)]
    outs = pl.pallas_call(
        functools.partial(pair_kernel, n_stats=len(stats), owners=owners, first_x=first_x),
        out_shape=out_shape,
        in_specs=[IN_VMEM for _ in args] + [pl.BlockSpec(memory_space=pl.ANY)],
        out_specs=[IN_VMEM for _ in out_shape],
        scratch_shapes=[
            pltpu.VMEM((2 * half, largest), jnp.bfloat16),
            pltpu.VMEM((2 * half, largest), jnp.bfloat16),
            pltpu.VMEM((cells, largest), jnp.bfloat16),
            pltpu.VMEM((cells, largest), jnp.bfloat16),
            pltpu.VMEM((cells, 2 * half), jnp.float32),
        ],
        compiler_params=pltpu.CompilerParams(vmem_limit_bytes=32 << 20),
        cost_estimate=COST,
        name="pair_grid",
    )(*args, after)
    return [o.reshape(rows, GZ_DEV, cells) for o in outs[:2]], outs[2:]


def from_other_phases(stats):
    size = lax.axis_size("phase")
    if size == 4:
        chip = lax.ppermute(stats, "phase", [(i, i ^ 2) for i in range(size)])
        core = lax.ppermute(stats, "phase", [(i, i ^ 1) for i in range(size)])
        return [core, chip, lax.ppermute(chip, "phase", [(i, i ^ 1) for i in range(size)])]
    return [
        lax.ppermute(stats, "phase", [(i, (i + k) % size) for i in range(size)])
        for k in range(1, size)]


def chain(chunk_of):
    size = lax.axis_size("space")
    me = lax.axis_index("space")
    up = down = None
    for step in range(1, size):
        send_up, send_down = chunk_of(size + me - step), chunk_of(me + step - size)
        up = send_up if up is None else up + send_up
        down = send_down if down is None else down + send_down
        up = lax.ppermute(up, "space", [(i, i + 1) for i in range(step)])
        down = lax.ppermute(down, "space", [(size - 1 - i, size - 2 - i) for i in range(step)])
    total = chunk_of(me)
    return total if up is None else total + up + down


FIRST = [(0, 1), (1, 3), (3, 2), (2, 0)]
SIDE = [(0, 1), (1, 0), (2, 3), (3, 2)]
ACROSS = [(0, 3), (3, 0), (1, 2), (2, 1)]


def flipped(first, second):
    def owners():
        me = lax.axis_index("space")
        return me ^ first, me ^ second

    return owners


def inner_device():
    me = lax.axis_index("space")
    return (me == 1) | (me == 2)


def join_kernel(own_ref, got_ref, out_ref):
    out_ref[...] = own_ref[...] + jnp.where(inner_device(), got_ref[...], 0.0)


def finish_kernel(*refs):
    out_ref = refs[-1]
    start = 0
    for piece in range(len(NEAR_SPLIT)):
        mine, side = refs[2 * piece:2 * piece + 2]
        cells = mine.shape[-1]
        out_ref[:, :, start:start + cells] = mine[...] + side[...]
        start += cells
    refs = refs[2 * len(NEAR_SPLIT):-1]
    start = 0
    for piece in range(len(SPLIT)):
        first, across = refs[2 * piece:2 * piece + 2]
        cells = first.shape[-1]
        out_ref[:, :, start:start + cells] += across[...] + jnp.where(inner_device(), 0.0, first[...])
        start += cells


def in_vmem(kernel, shape, args, out_spec):
    return pl.pallas_call(
        kernel, out_shape=jax.ShapeDtypeStruct(shape, jnp.float32),
        in_specs=[IN_VMEM for _ in args], out_specs=out_spec,
        compiler_params=pltpu.CompilerParams(vmem_limit_bytes=8 << 20))(*args)


def four_owners(pair_of):
    far, near = [], []
    threes, after = [], None
    for piece in range(len(SPLIT)):
        two, three = pair_of(flipped(2, 3), SPLIT, piece, after)
        far.append([lax.ppermute(two, "space", FIRST)])
        threes.append(three)
        after = two
    for piece in range(len(NEAR_SPLIT)):
        if piece < len(SPLIT):
            after = in_vmem(join_kernel, threes[piece].shape, (threes[piece], *far[piece]), IN_VMEM)
            far[piece].append(lax.ppermute(after, "space", ACROSS))
        one, mine = pair_of(flipped(1, 0), NEAR_SPLIT, piece, after)
        near.append([mine, lax.ppermute(one, "space", SIDE)])
    args = [a for pair in near + far for a in pair]
    return in_vmem(finish_kernel, mine.shape[:2] + (GX * GX,), args, pl.BlockSpec())


def local(intensity, image_grad, owner, coord_xy, coord_z):
    ph_dev, samples = intensity.shape
    size = lax.axis_size("space")
    stats = phase_stats(intensity)
    stats = [stats] + from_other_phases(stats)
    weights = plane_weights(coord_xy)
    raw = [intensity, image_grad, owner.reshape(1, samples), coord_z.reshape(1, samples)]
    prepared = []

    def pair_of(owners, split, piece, after=None):
        first_x, width = sum(split[:piece]), split[piece]
        after = stats[0] if after is None else after
        if prepared:
            return pair_grid(owners, [*prepared, *weights], first_x, width, after)[0]
        outs, kept = pair_grid(owners, [*raw, *stats, *weights], first_x, width, after, stats=stats)
        prepared.extend(kept)
        return outs

    if size == 4:
        grid = four_owners(pair_of)
    else:
        columns = []
        for piece in range(len(SPLIT)):
            chunks = []
            for start in range(0, size, 2):
                chunks += pair_of(lambda start=start: (start, min(start + 1, size - 1)), SPLIT, piece)
            table = jnp.stack(chunks)
            columns.append(chain(lambda j: lax.dynamic_index_in_dim(
                table, jnp.clip(j, 0, size - 1), 0, keepdims=False)))
        grid = jnp.concatenate(columns, axis=-1)
    return grid.reshape(3, ph_dev, GZ_DEV, GX * GX)


def solution(mesh):
    return jax.shard_map(
        local,
        mesh=mesh,
        in_specs=(
            P("phase", ("groups", "space")),
            P(None, "phase", ("groups", "space")),
            P(("groups", "space"), None),
            P(None, ("groups", "space")),
            P(("groups", "space")),
        ),
        out_specs=P("groups", "phase", "space", None),
        check_vma=False,
    )
```
